1024 devices in a mesh: context: 64 (over z, core), tensor: 16 (over x, y).
Axes of the slice: x: 4, y: 4, z: 32, core: 2. Of those that a mesh axis runs over, the one named last changes fastest.
Arguments:
- tokens: bfloat16 [16384, 4096], P(('context', 'tensor')), may hold values from -6 to 6
- norm_gain: float32 [4096], replicated, may hold values from 0.1 to 1.9
- w_qkv: bfloat16 [4096, 3, 4096], P(None, None, 'tensor'), may hold values from -0.09375 to 0.09375
- head_gain: float32 [4096], P('tensor'), may hold values from 0.1 to 1.9
- w_out: bfloat16 [4096, 4096], P('tensor'), may hold values from -0.09375 to 0.09375
Outputs:
- layer_out: bfloat16 [16384, 4096], P(('context', 'tensor'))
The draws below stay inside these ranges and needn't reach their ends.
All inputs are finite; a program needn't handle non-finite values.
Results may differ from the reference program's by a relative error of at most 0.0088.
Values may be sent and summed in bfloat16 or wider, within the bound.
No kernel may reach another device: no remote copies, remote signals or barrier semaphores. Data moves between devices by JAX's collectives and lax.ppermute only.
A program may use at most 64 MiB of HBM per device.

```python
import jax
import jax.numpy as jnp
from jax import lax

D = 4096
H = 32
HD = 128
TOK_DEV = 256
TOKENS = 16384
N_CONTEXT = 64


def level_of(own_key, dims, shards, least, high):
    loudness = 1.0
    for position, parts in shards:
        heights = jax.random.uniform(jax.random.fold_in(jax.random.fold_in(own_key, 6), position), (parts,), jnp.float32, least / len(shards), high / len(shards))
        loudness = loudness * jnp.repeat(jnp.exp(heights), dims[position] // parts).reshape((-1,) + (1,) * (len(dims) - 1 - position))
    return loudness


def scatter_about(stream_key, dims, deviation, most, cuts=(), held_as=jnp.bfloat16):
    drawn = deviation * jax.random.normal(stream_key, dims, jnp.float32)
    if cuts:
        drawn = drawn * level_of(stream_key, dims, cuts, -0.22, 0.18)
    return jnp.clip(drawn, -most, most).astype(held_as)


def setup_inputs(seed: int = 0) -> dict:
    arg_keys = jax.random.split(jax.random.key(seed), 6)
    tokens = scatter_about(arg_keys[0], (TOKENS, D), 1.0, 6.0, ((0, 1024),))
    norm_gain = jnp.clip(1.0 + 0.18 * jax.random.normal(arg_keys[1], (D,), jnp.float32), 0.1, 1.9)
    w_qkv = scatter_about(arg_keys[2], (D, 3, H * HD), D ** -0.5, 0.09375, ((2, 16),))
    head_gain = jnp.clip(1.0 + 0.18 * jax.random.normal(arg_keys[3], (H * HD,), jnp.float32), 0.1, 1.9)
    w_out = scatter_about(arg_keys[4], (H * HD, D), (H * HD) ** -0.5, 0.09375, ((0, 16),))
    return dict(tokens=tokens, norm_gain=norm_gain, w_qkv=w_qkv, head_gain=head_gain, w_out=w_out)


def reference(tokens, norm_gain, w_qkv, head_gain, w_out):
    x32 = tokens.astype(jnp.float32)
    normed = (x32 * lax.rsqrt(lax.optimization_barrier(jnp.mean(x32 * x32, axis=-1, keepdims=True)) + 1e-05) * norm_gain).astype(jnp.bfloat16)
    proj = jnp.dot(normed, w_qkv.reshape(D, 3 * H * HD), preferred_element_type=jnp.float32).astype(jnp.bfloat16)
    proj = proj.reshape(N_CONTEXT, TOK_DEV, 3, H, HD)
    query = proj[:, :, 0]
    keys = proj[:, :, 1]
    values = proj[:, :, 2]
    block_state = jnp.einsum('cthd,cthe->chde', keys.astype(jnp.float32), values.astype(jnp.float32))
    summed = jnp.cumsum(block_state, axis=0)
    prefix = jnp.concatenate([jnp.zeros_like(summed[:1]), summed[:-1]], axis=0).astype(jnp.bfloat16)
    positions = jnp.arange(TOK_DEV)
    causal = positions[:, None] >= positions[None, :]

    def one_block(items):
        qb, kb, vb, pb = items
        scores = jnp.einsum('thd,shd->hts', qb.astype(jnp.float32), kb.astype(jnp.float32))
        scores = jnp.where(causal[None], scores, 0.0).astype(jnp.bfloat16)
        intra = jnp.einsum('hts,shd->thd', scores.astype(jnp.float32), vb.astype(jnp.float32))
        inter = jnp.einsum('thd,hde->the', qb.astype(jnp.float32), pb.astype(jnp.float32))
        attended = intra + inter
        scale = lax.rsqrt(lax.optimization_barrier(jnp.mean(attended * attended, axis=-1, keepdims=True)) + 1e-05)
        flat = (attended * scale).reshape(TOK_DEV, H * HD) * head_gain
        return flat.astype(jnp.bfloat16)
    head_out = lax.map(one_block, (query, keys, values, prefix)).reshape(TOKENS, H * HD)
    result = jnp.dot(head_out, w_out, preferred_element_type=jnp.float32)
    return (x32 + result).astype(jnp.bfloat16)
```

```python
import jax
import jax.numpy as jnp
from jax import lax
from jax.sharding import Mesh
from jax.sharding import PartitionSpec as P

HD = 128
SIDE = 4
NEAR = 4
PLANE = ("core", "x", "y")
ALL = ("zh", "zl", "core", "x", "y")


def spot(core, bx, by, px, py):
    x, y = (core + 2 * bx + px) % SIDE, (core + 2 * by + py) % SIDE
    return core * SIDE * SIDE + x * SIDE + y


BITS = [(a, b) for a in range(2) for b in range(2)]
SQUARES = [[spot(c, bx, by, px, py) for px, py in BITS] for c in range(2) for bx, by in BITS]
CROSSES = [
    [spot(c, bx, by, (bx + jx) % 2, (by + jy) % 2) for bx, by in BITS]
    for c in range(2)
    for jx, jy in BITS
]


def swap(value, axes, groups=None):
    return lax.all_to_all(
        value, axes, split_axis=0, concat_axis=0, tiled=True, axis_index_groups=groups
    )


def norm_rows(rows, norm_gain):
    x32 = rows.astype(jnp.float32)
    scale = lax.rsqrt(jnp.mean(x32 * x32, axis=-1, keepdims=True) + 1e-05)
    return (x32 * scale * norm_gain).astype(jnp.bfloat16)


def gather_rows(rows):
    n, width = rows.shape
    for groups in (SQUARES, CROSSES):
        copies = jnp.broadcast_to(rows[None], (4,) + rows.shape)
        rows = swap(copies, PLANE, groups).reshape(4 * rows.shape[0], width)
    return rows


def scatter_sum(terms):
    for groups in (CROSSES, SQUARES):
        parts = terms.astype(jnp.bfloat16).reshape(4, terms.shape[0] // 4, terms.shape[1])
        parts = swap(parts, PLANE, groups).astype(jnp.float32)
        terms = (parts[0] + parts[1]) + (parts[2] + parts[3])
    return terms


def row_places(count):
    part = count // (SIDE * SIDE)
    i = lax.iota(jnp.int32, count)
    core = lax.axis_index("core")
    slot = i // part
    bx, by, px, py = slot // 8, slot // 4 % 2, slot // 2 % 2, slot % 2
    x, y = (core + 2 * bx + px) % SIDE, (core + 2 * by + py) % SIDE
    return (x * SIDE + y) * part + i % part


def earlier_sum(state):
    members = lax.axis_size("zl") * lax.axis_size("core")
    far = lax.axis_size("zh")
    shape = state.shape
    cut = swap(state.reshape(members, -1, HD), ("zl", "core"))
    before = [jnp.zeros_like(cut[0])]
    for m in range(members):
        before.append(before[-1] + cut[m])
    total = before.pop().astype(jnp.bfloat16)
    totals = swap(jnp.broadcast_to(total[None], (far,) + total.shape), ("zh",))
    mine = lax.axis_index("zh")
    reached = lax.broadcasted_iota(jnp.int32, (far, 1, 1), 0) < mine
    base = jnp.sum(jnp.where(reached, totals.astype(jnp.float32), 0.0), axis=0)
    prefix = jnp.stack([b + base for b in before]).astype(jnp.bfloat16)
    return swap(prefix, ("zl", "core")).reshape(shape)


def local(tokens, norm_gain, w_qkv, head_gain, w_out):
    heads = w_qkv.shape[2] // HD
    gathered = gather_rows(norm_rows(tokens, norm_gain))
    rows = gathered.shape[0]
    proj = [
        jnp.dot(gathered, w_qkv[:, j], preferred_element_type=jnp.float32).astype(jnp.bfloat16)
        for j in range(3)
    ]
    query, keys, values = [[p[:, h * HD : (h + 1) * HD] for h in range(heads)] for p in proj]
    state = jnp.stack(
        [
            jnp.einsum("td,te->de", k, v, preferred_element_type=jnp.float32)
            for k, v in zip(keys, values)
        ]
    )
    prefix = earlier_sum(state)
    place = row_places(rows)
    causal = place[:, None] >= place[None, :]
    outs = []
    for h in range(heads):
        scores = jnp.einsum("td,sd->ts", query[h], keys[h], preferred_element_type=jnp.float32)
        scores = jnp.where(causal, scores, 0.0).astype(jnp.bfloat16)
        attended = jnp.dot(scores, values[h], preferred_element_type=jnp.float32) + jnp.dot(
            query[h], prefix[h], preferred_element_type=jnp.float32
        )
        scale = lax.rsqrt(jnp.mean(attended * attended, axis=-1, keepdims=True) + 1e-05)
        gain = head_gain[h * HD : (h + 1) * HD]
        outs.append((attended * scale * gain).astype(jnp.bfloat16))
    head_out = jnp.concatenate(outs, axis=1)
    terms = jnp.dot(head_out, w_out, preferred_element_type=jnp.float32)
    return (tokens.astype(jnp.float32) + scatter_sum(terms)).astype(jnp.bfloat16)


def solution(mesh):
    context = mesh.shape["context"]
    cut = Mesh(mesh.devices.reshape(context // (2 * NEAR), NEAR, 2, SIDE, SIDE), ALL)
    return jax.shard_map(
        local,
        mesh=cut,
        in_specs=(
            P(ALL, None),
            P(),
            P(None, None, ("x", "y")),
            P(("x", "y")),
            P(("x", "y"), None),
        ),
        out_specs=P(ALL, None),
        check_vma=False,
    )
```

```python
import jax
import jax.numpy as jnp
from jax import lax
from jax.experimental import pallas as pl
from jax.experimental.pallas import tpu as pltpu
from jax.sharding import Mesh
from jax.sharding import PartitionSpec as P

HD = 128
SIDE = 4
NEAR = 4
PLANE = ("core", "x", "y")
ALL = ("zh", "zl", "core", "x", "y")


def spot(core, bx, by, px, py):
    x, y = (core + 2 * bx + px) % SIDE, (core + 2 * by + py) % SIDE
    return core * SIDE * SIDE + x * SIDE + y


BITS = [(a, b) for a in range(2) for b in range(2)]
SQUARES = [[spot(c, bx, by, px, py) for px, py in BITS] for c in range(2) for bx, by in BITS]
CROSSES = [
    [spot(c, bx, by, (bx + jx) % 2, (by + jy) % 2) for bx, by in BITS]
    for c in range(2)
    for jx, jy in BITS
]


def swap(value, axes, groups=None):
    return lax.all_to_all(
        value, axes, split_axis=0, concat_axis=0, tiled=True, axis_index_groups=groups
    )


def norm_kernel(rows_ref, gain_ref, out_ref):
    x32 = rows_ref[...].astype(jnp.float32)
    scale = lax.rsqrt(jnp.mean(x32 * x32, axis=-1, keepdims=True) + 1e-05)
    normed = (x32 * scale * gain_ref[...]).astype(jnp.bfloat16)
    for i in range(out_ref.shape[0]):
        out_ref[i] = normed


def norm_copies(rows, norm_gain):
    return pl.pallas_call(
        norm_kernel,
        out_shape=jax.ShapeDtypeStruct((4,) + rows.shape, jnp.bfloat16),
        in_specs=[pl.BlockSpec(memory_space=pltpu.VMEM)] * 2,
        out_specs=pl.BlockSpec(memory_space=pltpu.VMEM),
        name="norm_copies",
    )(rows, norm_gain[None])


def gather_rows(copies):
    width = copies.shape[2]
    rows = swap(copies, PLANE, SQUARES).reshape(-1, width)
    copies = jnp.broadcast_to(rows[None], (4,) + rows.shape)
    return swap(copies, PLANE, CROSSES).reshape(-1, width)


def scatter_sum(terms):
    for groups in (CROSSES, SQUARES):
        parts = terms.astype(jnp.bfloat16).reshape(4, terms.shape[0] // 4, terms.shape[1])
        a, b, c, d = [p.astype(jnp.float32) for p in swap(parts, PLANE, groups)]
        terms = (a + b) + (c + d)
    return terms


def row_places(count):
    part = count // (SIDE * SIDE)
    i = lax.iota(jnp.int32, count)
    core = lax.axis_index("core")
    slot = i // part
    bx, by, px, py = slot // 8, slot // 4 % 2, slot // 2 % 2, slot % 2
    x, y = (core + 2 * bx + px) % SIDE, (core + 2 * by + py) % SIDE
    return (x * SIDE + y) * part + i % part


def earlier_masks():
    far, members = lax.axis_size("zh"), lax.axis_size("zl") * lax.axis_size("core")
    group = lax.broadcasted_iota(jnp.int32, (far, 1, HD), 0)
    to = lax.broadcasted_iota(jnp.int32, (members, members, 1, HD), 0)
    since = lax.broadcasted_iota(jnp.int32, (members, members, 1, HD), 1)
    return (group < lax.axis_index("zh")).astype(jnp.float32), (since < to).astype(jnp.float32)


def earlier_sum(state, reached, lower):
    shape, far, members = state.shape, reached.shape[0], lower.shape[0]
    cut = swap(state.reshape(members, -1, HD), ("zl", "core"))
    total = jnp.sum(cut, axis=0).astype(jnp.bfloat16)
    before = jnp.sum(lower * cut[None], axis=1)
    before, total = lax.optimization_barrier((before, total))
    totals = swap(jnp.broadcast_to(total[None], (far,) + total.shape), ("zh",))
    base = jnp.sum(reached * totals.astype(jnp.float32), axis=0)
    prefix = (before + base).astype(jnp.bfloat16)
    return swap(prefix, ("zl", "core")).reshape(shape)


def local(tokens, norm_gain, w_qkv, head_gain, w_out):
    heads = w_qkv.shape[2] // HD
    reached, lower = earlier_masks()
    place = row_places(tokens.shape[0] * SIDE * SIDE)
    gains = [head_gain[h * HD : (h + 1) * HD] for h in range(heads)]
    copies, reached, lower, place, gains = lax.optimization_barrier(
        (norm_copies(tokens, norm_gain), reached, lower, place, gains)
    )
    gathered = gather_rows(copies)
    proj = [
        jnp.dot(gathered, w_qkv[:, j], preferred_element_type=jnp.float32).astype(jnp.bfloat16)
        for j in range(3)
    ]
    proj = lax.optimization_barrier(proj)
    query, keys, values = [[p[:, h * HD : (h + 1) * HD] for h in range(heads)] for p in proj]
    state = jnp.stack(
        [
            jnp.einsum("td,te->de", k, v, preferred_element_type=jnp.float32)
            for k, v in zip(keys, values)
        ]
    )
    prefix = earlier_sum(state, reached, lower)
    causal = place[:, None] >= place[None, :]
    outs = []
    for h in range(heads):
        scores = jnp.einsum("td,sd->ts", query[h], keys[h], preferred_element_type=jnp.float32)
        scores = jnp.where(causal, scores, 0.0).astype(jnp.bfloat16)
        attended = jnp.dot(scores, values[h], preferred_element_type=jnp.float32) + jnp.dot(
            query[h], prefix[h], preferred_element_type=jnp.float32
        )
        scale = lax.rsqrt(jnp.mean(attended * attended, axis=-1, keepdims=True) + 1e-05)
        outs.append((attended * scale * gains[h]).astype(jnp.bfloat16))
    head_out = jnp.concatenate(outs, axis=1)
    terms = jnp.dot(head_out, w_out, preferred_element_type=jnp.float32)
    return (tokens.astype(jnp.float32) + scatter_sum(terms)).astype(jnp.bfloat16)


def solution(mesh):
    context = mesh.shape["context"]
    cut = Mesh(mesh.devices.reshape(context // (2 * NEAR), NEAR, 2, SIDE, SIDE), ALL)
    return jax.shard_map(
        local,
        mesh=cut,
        in_specs=(
            P(ALL, None),
            P(),
            P(None, None, ("x", "y")),
            P(("x", "y")),
            P(("x", "y"), None),
        ),
        out_specs=P(ALL, None),
        check_vma=False,
    )
```

```python
import jax
import jax.numpy as jnp
from jax import lax
from jax.experimental import pallas as pl
from jax.experimental.pallas import tpu as pltpu
from jax.sharding import Mesh
from jax.sharding import PartitionSpec as P

HD = 128
SIDE = 4
NEAR = 4
PLANE = ("core", "x", "y")
ALL = ("zh", "zl", "core", "x", "y")


def spot(core, bx, by, px, py):
    x, y = (core + 2 * bx + px) % SIDE, (core + 2 * by + py) % SIDE
    return core * SIDE * SIDE + x * SIDE + y


BITS = [(a, b) for a in range(2) for b in range(2)]
SQUARES = [[spot(c, bx, by, px, py) for px, py in BITS] for c in range(2) for bx, by in BITS]
CROSSES = [
    [spot(c, bx, by, (bx + jx) % 2, (by + jy) % 2) for bx, by in BITS]
    for c in range(2)
    for jx, jy in BITS
]

WHOLE = [[spot(c, *far, *near) for far in BITS for near in BITS] for c in range(2)]


def swap(value, axes, groups=None):
    return lax.all_to_all(
        value, axes, split_axis=0, concat_axis=0, tiled=True, axis_index_groups=groups
    )


def norm_kernel(rows_ref, gain_ref, out_ref):
    x32 = rows_ref[...].astype(jnp.float32)
    scale = lax.rsqrt(jnp.mean(x32 * x32, axis=-1, keepdims=True) + 1e-05)
    out_ref[...] = (x32 * scale * gain_ref[...]).astype(jnp.bfloat16)


def norm_rows(rows, norm_gain):
    return pl.pallas_call(
        norm_kernel,
        out_shape=jax.ShapeDtypeStruct(rows.shape, jnp.bfloat16),
        in_specs=[pl.BlockSpec(memory_space=pltpu.VMEM)] * 2,
        out_specs=pl.BlockSpec(memory_space=pltpu.VMEM),
        name="norm_rows",
    )(rows, norm_gain[None])


def gather_rows(rows):
    for groups in (SQUARES, CROSSES):
        copies = jnp.broadcast_to(rows[None], (4,) + rows.shape)
        rows = swap(copies, PLANE, groups).reshape(-1, rows.shape[1])
    return rows


def scatter_sum(terms):
    chips = SIDE * SIDE
    parts = terms.astype(jnp.bfloat16).reshape(chips, terms.shape[0] // chips, terms.shape[1])
    parts = [p.astype(jnp.float32) for p in swap(parts, PLANE, WHOLE)]
    while len(parts) > 1:
        parts = [a + b for a, b in zip(parts[::2], parts[1::2])]
    return parts[0]


def row_places(count):
    part = count // (SIDE * SIDE)
    i = lax.iota(jnp.int32, count)
    core = lax.axis_index("core")
    slot = i // part
    bx, by, px, py = slot // 8, slot // 4 % 2, slot // 2 % 2, slot % 2
    x, y = (core + 2 * bx + px) % SIDE, (core + 2 * by + py) % SIDE
    return (x * SIDE + y) * part + i % part


def earlier_masks():
    far, members = lax.axis_size("zh"), lax.axis_size("zl") * lax.axis_size("core")
    group = lax.broadcasted_iota(jnp.int32, (far, 1, HD), 0)
    to = lax.broadcasted_iota(jnp.int32, (members, members, 1, HD), 0)
    since = lax.broadcasted_iota(jnp.int32, (members, members, 1, HD), 1)
    return (group < lax.axis_index("zh")).astype(jnp.float32), (since < to).astype(jnp.float32)


def earlier_sum(state, reached, lower):
    shape, far, members = state.shape, reached.shape[0], lower.shape[0]
    cut = state.astype(jnp.bfloat16).reshape(members, -1, HD)
    cut = swap(cut, ("zl", "core")).astype(jnp.float32)
    total = jnp.sum(cut, axis=0).astype(jnp.bfloat16)
    before = jnp.sum(lower * cut[None], axis=1)
    before, total = lax.optimization_barrier((before, total))
    totals = swap(jnp.broadcast_to(total[None], (far,) + total.shape), ("zh",))
    base = jnp.sum(reached * totals.astype(jnp.float32), axis=0)
    prefix = (before + base).astype(jnp.bfloat16)
    return swap(prefix, ("zl", "core")).reshape(shape)


def local(tokens, norm_gain, w_qkv, head_gain, w_out):
    heads = w_qkv.shape[2] // HD
    reached, lower = earlier_masks()
    place = row_places(tokens.shape[0] * SIDE * SIDE)
    normed, reached, lower, place = lax.optimization_barrier(
        (norm_rows(tokens, norm_gain), reached, lower, place)
    )
    gathered = gather_rows(normed)
    proj = [
        jnp.dot(gathered, w_qkv[:, j], preferred_element_type=jnp.float32).astype(jnp.bfloat16)
        for j in range(3)
    ]
    proj = lax.optimization_barrier(proj)
    query, keys, values = [[p[:, h * HD : (h + 1) * HD] for h in range(heads)] for p in proj]
    state = jnp.stack(
        [
            jnp.einsum("td,te->de", k, v, preferred_element_type=jnp.float32)
            for k, v in zip(keys, values)
        ]
    )
    prefix, gains = lax.optimization_barrier((earlier_sum(state, reached, lower), head_gain))
    causal = place[:, None] >= place[None, :]
    outs = []
    for h in range(heads):
        scores = jnp.einsum("td,sd->ts", query[h], keys[h], preferred_element_type=jnp.float32)
        scores = jnp.where(causal, scores, 0.0).astype(jnp.bfloat16)
        attended = jnp.dot(scores, values[h], preferred_element_type=jnp.float32) + jnp.dot(
            query[h], prefix[h], preferred_element_type=jnp.float32
        )
        scale = lax.rsqrt(jnp.mean(attended * attended, axis=-1, keepdims=True) + 1e-05)
        outs.append((attended * scale * gains[h * HD : (h + 1) * HD]).astype(jnp.bfloat16))
    head_out = jnp.concatenate(outs, axis=1)
    terms = jnp.dot(head_out, w_out, preferred_element_type=jnp.float32)
    return (tokens.astype(jnp.float32) + scatter_sum(terms)).astype(jnp.bfloat16)


def solution(mesh):
    context = mesh.shape["context"]
    cut = Mesh(mesh.devices.reshape(context // (2 * NEAR), NEAR, 2, SIDE, SIDE), ALL)
    return jax.shard_map(
        local,
        mesh=cut,
        in_specs=(
            P(ALL, None),
            P(),
            P(None, None, ("x", "y")),
            P(("x", "y")),
            P(("x", "y"), None),
        ),
        out_specs=P(ALL, None),
        check_vma=False,
    )
```

```python
import jax
import jax.numpy as jnp
from jax import lax
from jax.sharding import Mesh
from jax.sharding import PartitionSpec as P

HD = 128
SIDE = 4
NEAR = 4
PLANE = ("core", "x", "y")
ALL = ("zh", "zl", "core", "x", "y")


def spot(core, bx, by, px, py):
    x, y = (core + 2 * bx + px) % SIDE, (core + 2 * by + py) % SIDE
    return core * SIDE * SIDE + x * SIDE + y


BITS = [(a, b) for a in range(2) for b in range(2)]
SQUARES = [[spot(c, bx, by, px, py) for px, py in BITS] for c in range(2) for bx, by in BITS]
CROSSES = [
    [spot(c, bx, by, (bx + jx) % 2, (by + jy) % 2) for bx, by in BITS]
    for c in range(2)
    for jx, jy in BITS
]


def swap(value, axes, groups=None):
    return lax.all_to_all(
        value, axes, split_axis=0, concat_axis=0, tiled=True, axis_index_groups=groups
    )


def norm_rows(rows, norm_gain):
    x32 = rows.astype(jnp.float32)
    scale = lax.rsqrt(jnp.mean(x32 * x32, axis=-1, keepdims=True) + 1e-05)
    return (x32 * scale * norm_gain).astype(jnp.bfloat16)


def spread(rows, groups):
    copies = jnp.broadcast_to(rows[None], (4,) + rows.shape)
    return swap(copies, PLANE, groups).reshape(-1, rows.shape[1])


def scatter_sum(terms):
    for groups in (CROSSES, SQUARES):
        parts = terms.astype(jnp.bfloat16).reshape(4, terms.shape[0] // 4, terms.shape[1])
        a, b, c, d = [p.astype(jnp.float32) for p in swap(parts, PLANE, groups)]
        terms = (a + b) + (c + d)
    return terms


def row_places(count):
    part = count // (SIDE * SIDE)
    i = lax.iota(jnp.int32, count)
    core = lax.axis_index("core")
    slot = i // part
    bx, by, px, py = slot // 8, slot // 4 % 2, slot // 2 % 2, slot % 2
    x, y = (core + 2 * bx + px) % SIDE, (core + 2 * by + py) % SIDE
    return (x * SIDE + y) * part + i % part


def earlier_masks():
    far, members = lax.axis_size("zh"), lax.axis_size("zl") * lax.axis_size("core")
    group = lax.broadcasted_iota(jnp.int32, (far, 1, HD), 0)
    to = lax.broadcasted_iota(jnp.int32, (members, members, 1, HD), 0)
    since = lax.broadcasted_iota(jnp.int32, (members, members, 1, HD), 1)
    return (group < lax.axis_index("zh")).astype(jnp.float32), (since < to).astype(jnp.float32)


def earlier_sum(state, reached, lower):
    shape, far, members = state.shape, reached.shape[0], lower.shape[0]
    cut = state.astype(jnp.bfloat16).reshape(members, -1, HD)
    cut = swap(cut, ("zl", "core")).astype(jnp.float32)
    total = jnp.sum(cut, axis=0).astype(jnp.bfloat16)
    before = jnp.sum(lower * cut[None], axis=1)
    before, total = lax.optimization_barrier((before, total))
    totals = swap(jnp.broadcast_to(total[None], (far,) + total.shape), ("zh",))
    base = jnp.sum(reached * totals.astype(jnp.float32), axis=0)
    prefix = (before + base).astype(jnp.bfloat16)
    return swap(prefix, ("zl", "core")).reshape(shape)


def local(tokens, norm_gain, w_qkv, head_gain, w_out):
    heads = w_qkv.shape[2] // HD
    reached, lower = earlier_masks()
    place = row_places(tokens.shape[0] * SIDE * SIDE)
    own, reached, lower, place = lax.optimization_barrier((tokens, reached, lower, place))
    square = spread(own, SQUARES)
    gathered = spread(norm_rows(square, norm_gain), CROSSES)
    proj = [
        jnp.dot(gathered, w_qkv[:, j], preferred_element_type=jnp.float32).astype(jnp.bfloat16)
        for j in range(3)
    ]
    proj = lax.optimization_barrier(proj)
    query, keys, values = [[p[:, h * HD : (h + 1) * HD] for h in range(heads)] for p in proj]
    state = jnp.stack(
        [
            jnp.einsum("td,te->de", k, v, preferred_element_type=jnp.float32)
            for k, v in zip(keys, values)
        ]
    )
    prefix, gains = lax.optimization_barrier((earlier_sum(state, reached, lower), head_gain))
    causal = place[:, None] >= place[None, :]
    outs = []
    for h in range(heads):
        scores = jnp.einsum("td,sd->ts", query[h], keys[h], preferred_element_type=jnp.float32)
        scores = jnp.where(causal, scores, 0.0).astype(jnp.bfloat16)
        attended = jnp.dot(scores, values[h], preferred_element_type=jnp.float32) + jnp.dot(
            query[h], prefix[h], preferred_element_type=jnp.float32
        )
        scale = lax.rsqrt(jnp.mean(attended * attended, axis=-1, keepdims=True) + 1e-05)
        outs.append((attended * scale * gains[h * HD : (h + 1) * HD]).astype(jnp.bfloat16))
    head_out = jnp.concatenate(outs, axis=1)
    terms = jnp.dot(head_out, w_out, preferred_element_type=jnp.float32)
    return (tokens.astype(jnp.float32) + scatter_sum(terms)).astype(jnp.bfloat16)


def solution(mesh):
    context = mesh.shape["context"]
    cut = Mesh(mesh.devices.reshape(context // (2 * NEAR), NEAR, 2, SIDE, SIDE), ALL)
    return jax.shard_map(
        local,
        mesh=cut,
        in_specs=(
            P(ALL, None),
            P(),
            P(None, None, ("x", "y")),
            P(("x", "y")),
            P(("x", "y"), None),
        ),
        out_specs=P(ALL, None),
        check_vma=False,
    )
```

```python
import jax
import jax.numpy as jnp
from jax import lax
from jax.sharding import Mesh
from jax.sharding import PartitionSpec as P


HD = 128
SIDE = 4
NEAR = 4
PLANE = ("core", "x", "y")
ALL = ("zh", "zl", "core", "x", "y")


def spot(core, bx, by, px, py):
    x, y = (core + 2 * bx + px) % SIDE, (core + 2 * by + py) % SIDE
    return core * SIDE * SIDE + x * SIDE + y


BITS = [(a, b) for a in range(2) for b in range(2)]
SQUARES = [[spot(c, bx, by, px, py) for px, py in BITS] for c in range(2) for bx, by in BITS]
CROSSES = [
    [spot(c, bx, by, (bx + jx) % 2, (by + jy) % 2) for bx, by in BITS]
    for c in range(2)
    for jx, jy in BITS
]


FLIPS = BITS[1:]
FETCHED = 2


def fetch(value, ax, ay):
    pairs = []
    for c in range(2):
        for jx, jy in BITS:
            for bx, by in BITS:
                tx, ty = bx ^ ax, by ^ ay
                source = spot(c, bx, by, (bx + jx) % 2, (by + jy) % 2)
                pairs.append((source, spot(c, tx, ty, (tx + jx) % 2, (ty + jy) % 2)))
    return lax.ppermute(value, PLANE, pairs)


def partner_slots():
    core = lax.axis_index("core")
    bx = ((lax.axis_index("x") - core) & (SIDE - 1)) >> 1
    by = ((lax.axis_index("y") - core) & (SIDE - 1)) >> 1
    return [((2 * bx + by) ^ k).astype(jnp.uint32) for k in range(4)]


def swap(value, axes, groups=None):
    return lax.all_to_all(
        value, axes, split_axis=0, concat_axis=0, tiled=True, axis_index_groups=groups
    )


def norm_rows(rows, norm_gain):
    x32 = rows.astype(jnp.float32)
    scale = lax.rsqrt(jnp.mean(x32 * x32, axis=-1, keepdims=True) + 1e-05)
    return (x32 * scale * norm_gain).astype(jnp.bfloat16)


def spread(rows, groups):
    copies = jnp.broadcast_to(rows[None], (4,) + rows.shape)
    return swap(copies, PLANE, groups).reshape(-1, rows.shape[1])


def stage_parts(terms):
    return terms.reshape(4, terms.shape[0] // 4, terms.shape[1])


def add_parts(parts):
    a, b, c, d = [p.astype(jnp.float32) for p in parts]
    return (a + b) + (c + d)


def project_sum(head_out, w_out, fetched, slots):
    width = fetched[0].shape[1]
    terms = jnp.dot(head_out, w_out[:, width:], preferred_element_type=jnp.float32)
    rest = terms.shape[1]
    mixed = jnp.concatenate([terms.astype(jnp.bfloat16), head_out], axis=1)
    mixed = swap(stage_parts(mixed), PLANE, CROSSES)
    later = add_parts(mixed[:, :, :rest])
    heads = mixed[:, :, rest:]
    first = 0.0
    for slot, w in zip(slots, fetched):
        rows = lax.dynamic_index_in_dim(heads, slot, 0, keepdims=False)
        first = first + jnp.dot(rows, w, preferred_element_type=jnp.float32)
    terms = jnp.concatenate([first, later], axis=1).astype(jnp.bfloat16)
    return add_parts(swap(stage_parts(terms), PLANE, SQUARES))


def row_places(count):
    part = count // (SIDE * SIDE)
    i = lax.iota(jnp.int32, count)
    core = lax.axis_index("core")
    slot = i // part
    bx, by, px, py = slot // 8, slot // 4 % 2, slot // 2 % 2, slot % 2
    x, y = (core + 2 * bx + px) % SIDE, (core + 2 * by + py) % SIDE
    return (x * SIDE + y) * part + i % part


def earlier_masks():
    far, members = lax.axis_size("zh"), lax.axis_size("zl") * lax.axis_size("core")
    group = lax.broadcasted_iota(jnp.int32, (far, 1, HD), 0)
    to = lax.broadcasted_iota(jnp.int32, (members, members, 1, HD), 0)
    since = lax.broadcasted_iota(jnp.int32, (members, members, 1, HD), 1)
    return (group < lax.axis_index("zh")).astype(jnp.float32), (since < to).astype(jnp.float32)


def earlier_sum(state, reached, lower):
    shape, far, members = state.shape, reached.shape[0], lower.shape[0]
    cut = state.astype(jnp.bfloat16).reshape(members, -1, HD)
    cut = swap(cut, ("zl", "core")).astype(jnp.float32)
    total = jnp.sum(cut, axis=0).astype(jnp.bfloat16)
    before = jnp.sum(lower * cut[None], axis=1)
    before, total = lax.optimization_barrier((before, total))
    totals = swap(jnp.broadcast_to(total[None], (far,) + total.shape), ("zh",))
    base = jnp.sum(reached * totals.astype(jnp.float32), axis=0)
    prefix = (before + base).astype(jnp.bfloat16)
    return swap(prefix, ("zl", "core")).reshape(shape)


def layer(tokens, norm_gain, w_qkv, head_gain, w_out):
    heads = w_qkv.shape[2] // HD
    reached, lower = earlier_masks()
    place = row_places(tokens.shape[0] * SIDE * SIDE)
    columns = w_out[:, : w_out.shape[1] // FETCHED]
    own, reached, lower, place, slots = lax.optimization_barrier(
        (tokens, reached, lower, place, partner_slots())
    )
    fetched = [columns] + [fetch(columns, ax, ay) for ax, ay in FLIPS]
    square = spread(own, SQUARES)
    gathered = spread(norm_rows(square, norm_gain), CROSSES)
    proj = [
        jnp.dot(gathered, w_qkv[:, j], preferred_element_type=jnp.float32).astype(jnp.bfloat16)
        for j in range(3)
    ]
    proj = lax.optimization_barrier(proj)
    query, keys, values = [[p[:, h * HD : (h + 1) * HD] for h in range(heads)] for p in proj]
    state = jnp.stack(
        [
            jnp.einsum("td,te->de", k, v, preferred_element_type=jnp.float32)
            for k, v in zip(keys, values)
        ]
    )
    prefix, gains = lax.optimization_barrier((earlier_sum(state, reached, lower), head_gain))
    causal = place[:, None] >= place[None, :]
    outs = []
    for h in range(heads):
        scores = jnp.einsum("td,sd->ts", query[h], keys[h], preferred_element_type=jnp.float32)
        scores = jnp.where(causal, scores, 0.0).astype(jnp.bfloat16)
        attended = jnp.dot(scores, values[h], preferred_element_type=jnp.float32) + jnp.dot(
            query[h], prefix[h], preferred_element_type=jnp.float32
        )
        scale = lax.rsqrt(jnp.mean(attended * attended, axis=-1, keepdims=True) + 1e-05)
        outs.append((attended * scale * gains[h * HD : (h + 1) * HD]).astype(jnp.bfloat16))
    head_out = jnp.concatenate(outs, axis=1)
    summed = project_sum(head_out, w_out, fetched, slots)
    return (tokens.astype(jnp.float32) + summed).astype(jnp.bfloat16)


def solution(mesh):
    context = mesh.shape["context"]
    cut = Mesh(mesh.devices.reshape(context // (2 * NEAR), NEAR, 2, SIDE, SIDE), ALL)
    return jax.shard_map(
        layer,
        mesh=cut,
        in_specs=(
            P(ALL, None),
            P(),
            P(None, None, ("x", "y")),
            P(("x", "y")),
            P(("x", "y"), None),
        ),
        out_specs=P(ALL, None),
        check_vma=False,
    )
```

```python
import jax
import jax.numpy as jnp
from jax import lax
from jax.sharding import Mesh
from jax.sharding import PartitionSpec as P

HD = 128
SIDE = 4
NEAR = 4
PLANE = ("core", "x", "y")
ALL = ("zh", "zl", "core", "x", "y")


def spot(core, bx, by, px, py):
    x, y = (core + 2 * bx + px) % SIDE, (1 - core + 2 * by + py) % SIDE
    return core * SIDE * SIDE + x * SIDE + y


BITS = [(a, b) for a in range(2) for b in range(2)]
SQUARES = [[spot(c, bx, by, px, py) for px, py in BITS] for c in range(2) for bx, by in BITS]
CROSSES = [
    [spot(c, bx, by, (bx + jx) % 2, (by + jy) % 2) for bx, by in BITS]
    for c in range(2)
    for jx, jy in BITS
]


def swap(value, axes, groups=None):
    return lax.all_to_all(
        value, axes, split_axis=0, concat_axis=0, tiled=True, axis_index_groups=groups
    )


def norm_rows(rows, norm_gain):
    x32 = rows.astype(jnp.float32)
    scale = lax.rsqrt(jnp.mean(x32 * x32, axis=-1, keepdims=True) + 1e-05)
    return (x32 * scale * norm_gain).astype(jnp.bfloat16)


def spread(rows, groups):
    copies = jnp.broadcast_to(rows[None], (4,) + rows.shape)
    return swap(copies, PLANE, groups).reshape(-1, rows.shape[1])


def scatter_sum(terms):
    for groups in (CROSSES, SQUARES):
        parts = terms.astype(jnp.bfloat16).reshape(4, terms.shape[0] // 4, terms.shape[1])
        a, b, c, d = [p.astype(jnp.float32) for p in swap(parts, PLANE, groups)]
        terms = (a + b) + (c + d)
    return terms


def row_places(count):
    part = count // (SIDE * SIDE)
    i = lax.iota(jnp.int32, count)
    core = lax.axis_index("core")
    slot = i // part
    bx, by, px, py = slot // 8, slot // 4 % 2, slot // 2 % 2, slot % 2
    x, y = (core + 2 * bx + px) % SIDE, (1 - core + 2 * by + py) % SIDE
    return (x * SIDE + y) * part + i % part


def earlier_masks():
    far, members = lax.axis_size("zh"), lax.axis_size("zl") * lax.axis_size("core")
    group = lax.broadcasted_iota(jnp.int32, (far, 1, HD), 0)
    to = lax.broadcasted_iota(jnp.int32, (members, members, 1, HD), 0)
    since = lax.broadcasted_iota(jnp.int32, (members, members, 1, HD), 1)
    return (group < lax.axis_index("zh")).astype(jnp.float32), (since < to).astype(jnp.float32)


def earlier_sum(state, reached, lower):
    shape, far, members = state.shape, reached.shape[0], lower.shape[0]
    cut = state.astype(jnp.bfloat16).reshape(members, -1, HD)
    cut = swap(cut, ("zl", "core")).astype(jnp.float32)
    total = jnp.sum(cut, axis=0).astype(jnp.bfloat16)
    before = jnp.sum(lower * cut[None], axis=1)
    before, total = lax.optimization_barrier((before, total))
    totals = swap(jnp.broadcast_to(total[None], (far,) + total.shape), ("zh",))
    base = jnp.sum(reached * totals.astype(jnp.float32), axis=0)
    prefix = (before + base).astype(jnp.bfloat16)
    return swap(prefix, ("zl", "core")).reshape(shape)


def local(tokens, norm_gain, w_qkv, head_gain, w_out):
    heads = w_qkv.shape[2] // HD
    reached, lower = earlier_masks()
    place = row_places(tokens.shape[0] * SIDE * SIDE)
    own, reached, lower, place = lax.optimization_barrier((tokens, reached, lower, place))
    square = spread(own, SQUARES)
    gathered = spread(norm_rows(square, norm_gain), CROSSES)
    proj = [
        jnp.dot(gathered, w_qkv[:, j], preferred_element_type=jnp.float32).astype(jnp.bfloat16)
        for j in range(3)
    ]
    proj = lax.optimization_barrier(proj)
    query, keys, values = [[p[:, h * HD : (h + 1) * HD] for h in range(heads)] for p in proj]
    state = jnp.stack(
        [
            jnp.einsum("td,te->de", k, v, preferred_element_type=jnp.float32)
            for k, v in zip(keys, values)
        ]
    )
    prefix, gains = lax.optimization_barrier((earlier_sum(state, reached, lower), head_gain))
    causal = place[:, None] >= place[None, :]
    outs = []
    for h in range(heads):
        scores = jnp.einsum("td,sd->ts", query[h], keys[h], preferred_element_type=jnp.float32)
        scores = jnp.where(causal, scores, 0.0).astype(jnp.bfloat16)
        attended = jnp.dot(scores, values[h], preferred_element_type=jnp.float32) + jnp.dot(
            query[h], prefix[h], preferred_element_type=jnp.float32
        )
        scale = lax.rsqrt(jnp.mean(attended * attended, axis=-1, keepdims=True) + 1e-05)
        outs.append((attended * scale * gains[h * HD : (h + 1) * HD]).astype(jnp.bfloat16))
    head_out = jnp.concatenate(outs, axis=1)
    terms = jnp.dot(head_out, w_out, preferred_element_type=jnp.float32)
    return (tokens.astype(jnp.float32) + scatter_sum(terms)).astype(jnp.bfloat16)


def solution(mesh):
    context = mesh.shape["context"]
    cut = Mesh(mesh.devices.reshape(context // (2 * NEAR), NEAR, 2, SIDE, SIDE), ALL)
    return jax.shard_map(
        local,
        mesh=cut,
        in_specs=(
            P(ALL, None),
            P(),
            P(None, None, ("x", "y")),
            P(("x", "y")),
            P(("x", "y"), None),
        ),
        out_specs=P(ALL, None),
        check_vma=False,
    )
```

```python
import jax
import jax.numpy as jnp
from jax import lax
from jax.experimental import pallas as pl
from jax.experimental.pallas import tpu as pltpu
from jax.sharding import Mesh
from jax.sharding import PartitionSpec as P


HD = 128
SIDE = 4
NEAR = 4
PLANE = ("core", "x", "y")
ALL = ("zh", "zl", "core", "x", "y")


def spot(core, bx, by, px, py):
    x, y = (core + 2 * bx + px) % SIDE, (1 - core + 2 * by + py) % SIDE
    return core * SIDE * SIDE + x * SIDE + y


BITS = [(a, b) for a in range(2) for b in range(2)]
SQUARES = [[spot(c, bx, by, px, py) for px, py in BITS] for c in range(2) for bx, by in BITS]
CROSSES = [
    [spot(c, bx, by, (bx + jx) % 2, (by + jy) % 2) for bx, by in BITS]
    for c in range(2)
    for jx, jy in BITS
]


FLIPS = BITS[1:]
FETCHED = 2


def fetch(value, ax, ay):
    pairs = []
    for c in range(2):
        for jx, jy in BITS:
            for bx, by in BITS:
                tx, ty = bx ^ ax, by ^ ay
                source = spot(c, bx, by, (bx + jx) % 2, (by + jy) % 2)
                pairs.append((source, spot(c, tx, ty, (tx + jx) % 2, (ty + jy) % 2)))
    return lax.ppermute(value, PLANE, pairs)


def partner_slots():
    core = lax.axis_index("core")
    bx = ((lax.axis_index("x") - core) & (SIDE - 1)) >> 1
    by = ((lax.axis_index("y") - 1 + core) & (SIDE - 1)) >> 1
    return jnp.stack([(2 * bx + by) ^ k for k in range(4)])


def swap(value, axes, groups=None):
    return lax.all_to_all(
        value, axes, split_axis=0, concat_axis=0, tiled=True, axis_index_groups=groups
    )


def norm_rows(rows, norm_gain):
    x32 = rows.astype(jnp.float32)
    scale = lax.rsqrt(jnp.mean(x32 * x32, axis=-1, keepdims=True) + 1e-05)
    return (x32 * scale * norm_gain).astype(jnp.bfloat16)


def spread(rows, groups):
    copies = jnp.broadcast_to(rows[None], (4,) + rows.shape)
    return swap(copies, PLANE, groups).reshape(-1, rows.shape[1])


def stage_parts(terms):
    return terms.reshape(4, terms.shape[0] // 4, terms.shape[1])


def add_parts(parts):
    a, b, c, d = [p.astype(jnp.float32) for p in parts]
    return (a + b) + (c + d)


def products_kernel(slots_ref, heads_ref, *refs):
    total = 0.0
    for k, w_ref in enumerate(refs[:-1]):
        rows = heads_ref[slots_ref[k]]
        total += jnp.dot(rows, w_ref[...], preferred_element_type=jnp.float32)
    refs[-1][...] = total.astype(jnp.bfloat16)


def products(heads, slots, fetched):
    depth, width = fetched[0].shape
    tile = 512
    held = pl.BlockSpec(heads.shape, lambda i, s: (0, 0, 0))
    block = pl.BlockSpec((depth, tile), lambda i, s: (0, i))
    return pl.pallas_call(
        products_kernel,
        out_shape=jax.ShapeDtypeStruct((heads.shape[1], width), jnp.bfloat16),
        grid_spec=pltpu.PrefetchScalarGridSpec(
            num_scalar_prefetch=1,
            grid=(width // tile,),
            in_specs=[held] + [block] * 4,
            out_specs=pl.BlockSpec((heads.shape[1], tile), lambda i, s: (0, i)),
        ),
        name="products",
    )(slots, heads, *fetched)


def project_sum(head_out, w_out, fetched, slots):
    width = fetched[0].shape[1]
    terms = jnp.dot(head_out, w_out[:, width:], preferred_element_type=jnp.float32)
    rest = terms.shape[1]
    mixed = jnp.concatenate([terms.astype(jnp.bfloat16), head_out], axis=1)
    mixed, fetched = lax.optimization_barrier((mixed, fetched))
    mixed = swap(stage_parts(mixed), PLANE, CROSSES)
    later = add_parts(mixed[:, :, :rest])
    heads = mixed[:, :, rest:]
    first = products(heads, slots, fetched)
    later = later.astype(jnp.bfloat16)
    terms = jnp.concatenate([first, later], axis=1)
    return add_parts(swap(stage_parts(terms), PLANE, SQUARES))


def row_places(count):
    part = count // (SIDE * SIDE)
    i = lax.iota(jnp.int32, count)
    core = lax.axis_index("core")
    slot = i // part
    bx, by, px, py = slot // 8, slot // 4 % 2, slot // 2 % 2, slot % 2
    x, y = (core + 2 * bx + px) % SIDE, (1 - core + 2 * by + py) % SIDE
    return (x * SIDE + y) * part + i % part


def earlier_masks():
    far, members = lax.axis_size("zh"), lax.axis_size("zl") * lax.axis_size("core")
    group = lax.broadcasted_iota(jnp.int32, (far, 1, HD), 0)
    to = lax.broadcasted_iota(jnp.int32, (members, members, 1, HD), 0)
    since = lax.broadcasted_iota(jnp.int32, (members, members, 1, HD), 1)
    return (group < lax.axis_index("zh")).astype(jnp.float32), (since < to).astype(jnp.float32)


def earlier_sum(state, reached, lower, intra, w_out):
    shape, far, members = state.shape, reached.shape[0], lower.shape[0]
    cut = state.astype(jnp.bfloat16).reshape(members, -1, HD)
    cut = swap(cut, ("zl", "core")).astype(jnp.float32)
    total = jnp.sum(cut, axis=0).astype(jnp.bfloat16)
    before = jnp.sum(lower * cut[None], axis=1)
    before, total, w_out = lax.optimization_barrier((before, total, w_out))
    columns = w_out[:, : w_out.shape[1] // FETCHED]
    fetched = [columns] + [fetch(columns, ax, ay) for ax, ay in FLIPS]
    totals = swap(jnp.broadcast_to(total[None], (far,) + total.shape), ("zh",))
    base = jnp.sum(reached * totals.astype(jnp.float32), axis=0)
    prefix = (before + base).astype(jnp.bfloat16)
    prefix, intra = lax.optimization_barrier((prefix, intra))
    return swap(prefix, ("zl", "core")).reshape(shape), intra, fetched


def layer(tokens, norm_gain, w_qkv, head_gain, w_out):
    heads = w_qkv.shape[2] // HD
    reached, lower = earlier_masks()
    place = row_places(tokens.shape[0] * SIDE * SIDE)
    own, reached, lower, place, slots = lax.optimization_barrier(
        (tokens, reached, lower, place, partner_slots())
    )
    square = spread(own, SQUARES)
    gathered = spread(norm_rows(square, norm_gain), CROSSES)
    proj = [
        jnp.dot(gathered, w_qkv[:, j], preferred_element_type=jnp.float32).astype(jnp.bfloat16)
        for j in range(3)
    ]
    proj = lax.optimization_barrier(proj)
    query, keys, values = [[p[:, h * HD : (h + 1) * HD] for h in range(heads)] for p in proj]
    state = jnp.stack(
        [
            jnp.einsum("td,te->de", k, v, preferred_element_type=jnp.float32)
            for k, v in zip(keys, values)
        ]
    )
    causal = place[:, None] >= place[None, :]
    intra = []
    for h in range(heads):
        scores = jnp.einsum("td,sd->ts", query[h], keys[h], preferred_element_type=jnp.float32)
        scores = jnp.where(causal, scores, 0.0).astype(jnp.bfloat16)
        intra.append(jnp.dot(scores, values[h], preferred_element_type=jnp.float32))
    prefix, intra, fetched = earlier_sum(state, reached, lower, intra, w_out)
    prefix, gains = lax.optimization_barrier((prefix, head_gain))
    outs = []
    for h in range(heads):
        inter = jnp.dot(query[h], prefix[h], preferred_element_type=jnp.float32)
        attended = intra[h] + inter
        scale = lax.rsqrt(jnp.mean(attended * attended, axis=-1, keepdims=True) + 1e-05)
        outs.append((attended * scale * gains[h * HD : (h + 1) * HD]).astype(jnp.bfloat16))
    head_out = jnp.concatenate(outs, axis=1)
    summed = project_sum(head_out, w_out, fetched, slots)
    return (tokens.astype(jnp.float32) + summed).astype(jnp.bfloat16)


def solution(mesh):
    context = mesh.shape["context"]
    cut = Mesh(mesh.devices.reshape(context // (2 * NEAR), NEAR, 2, SIDE, SIDE), ALL)
    return jax.shard_map(
        layer,
        mesh=cut,
        in_specs=(
            P(ALL, None),
            P(),
            P(None, None, ("x", "y")),
            P(("x", "y")),
            P(("x", "y"), None),
        ),
        out_specs=P(ALL, None),
        check_vma=False,
    )
```

```python
import jax
import jax.numpy as jnp
from jax import lax
from jax.sharding import Mesh
from jax.sharding import PartitionSpec as P

HD = 128
SIDE = 4
NEAR = 4
PLANE = ("core", "x", "y")
ALL = ("zh", "zl", "core", "x", "y")


def spot(core, bx, by, px, py):
    x, y = (core + 2 * bx + px) % SIDE, (1 - core + 2 * by + py) % SIDE
    return core * SIDE * SIDE + x * SIDE + y


BITS = [(a, b) for a in range(2) for b in range(2)]
SQUARES = [[spot(c, bx, by, px, py) for px, py in BITS] for c in range(2) for bx, by in BITS]
CROSSES = [
    [spot(c, bx, by, (bx + jx) % 2, (by + jy) % 2) for bx, by in BITS]
    for c in range(2)
    for jx, jy in BITS
]


def swap(value, axes, groups=None):
    return lax.all_to_all(
        value, axes, split_axis=0, concat_axis=0, tiled=True, axis_index_groups=groups
    )


def norm_rows(rows, norm_gain):
    x32 = rows.astype(jnp.float32)
    scale = lax.rsqrt(jnp.mean(x32 * x32, axis=-1, keepdims=True) + 1e-05)
    return (x32 * scale * norm_gain).astype(jnp.bfloat16)


def spread(rows, groups):
    copies = jnp.broadcast_to(rows[None], (4,) + rows.shape)
    return swap(copies, PLANE, groups).reshape(-1, rows.shape[1])


def scatter_sum(terms):
    for groups in (CROSSES, SQUARES):
        parts = terms.astype(jnp.bfloat16).reshape(4, terms.shape[0] // 4, terms.shape[1])
        a, b, c, d = [p.astype(jnp.float32) for p in swap(parts, PLANE, groups)]
        terms = (a + b) + (c + d)
    return terms


def row_places(count):
    part = count // (SIDE * SIDE)
    i = lax.iota(jnp.int32, count)
    core = lax.axis_index("core")
    slot = i // part
    bx, by, px, py = slot // 8, slot // 4 % 2, slot // 2 % 2, slot % 2
    x, y = (core + 2 * bx + px) % SIDE, (1 - core + 2 * by + py) % SIDE
    return (x * SIDE + y) * part + i % part


def earlier_masks():
    far, members = lax.axis_size("zh"), lax.axis_size("zl") * lax.axis_size("core")
    group = lax.broadcasted_iota(jnp.int32, (far, 1, HD), 0)
    to = lax.broadcasted_iota(jnp.int32, (members, members, 1, HD), 0)
    since = lax.broadcasted_iota(jnp.int32, (members, members, 1, HD), 1)
    return (group < lax.axis_index("zh")).astype(jnp.float32), (since < to).astype(jnp.float32)


def earlier_sum(state, reached, lower):
    shape, far, members = state.shape, reached.shape[0], lower.shape[0]
    cut = state.astype(jnp.bfloat16).reshape(members, -1, HD)
    cut = swap(cut, ("zl", "core")).astype(jnp.float32)
    total = jnp.sum(cut, axis=0).astype(jnp.bfloat16)
    before = jnp.sum(lower * cut[None], axis=1)
    before, total = lax.optimization_barrier((before, total))
    totals = swap(jnp.broadcast_to(total[None], (far,) + total.shape), ("zh",))
    base = jnp.sum(reached * totals.astype(jnp.float32), axis=0)
    prefix = (before + base).astype(jnp.bfloat16)
    return swap(prefix, ("zl", "core")).reshape(shape)


def local(tokens, norm_gain, w_qkv, head_gain, w_out):
    heads = w_qkv.shape[2] // HD
    reached, lower = earlier_masks()
    place = row_places(tokens.shape[0] * SIDE * SIDE)
    own, reached, lower, place = lax.optimization_barrier((tokens, reached, lower, place))
    square = spread(own, SQUARES)
    gathered = spread(norm_rows(square, norm_gain), CROSSES)
    flat = jnp.einsum("tk,kjn->jtn", gathered, w_qkv, preferred_element_type=jnp.float32)
    proj = lax.optimization_barrier(flat.astype(jnp.bfloat16))
    query, keys, values = [[p[:, h * HD : (h + 1) * HD] for h in range(heads)] for p in proj]
    state = jnp.stack(
        [
            jnp.einsum("td,te->de", k, v, preferred_element_type=jnp.float32)
            for k, v in zip(keys, values)
        ]
    )
    prefix, gains = lax.optimization_barrier((earlier_sum(state, reached, lower), head_gain))
    causal = place[:, None] >= place[None, :]
    outs = []
    for h in range(heads):
        scores = jnp.einsum("td,sd->ts", query[h], keys[h], preferred_element_type=jnp.float32)
        scores = jnp.where(causal, scores, 0.0).astype(jnp.bfloat16)
        attended = jnp.dot(scores, values[h], preferred_element_type=jnp.float32) + jnp.dot(
            query[h], prefix[h], preferred_element_type=jnp.float32
        )
        scale = lax.rsqrt(jnp.mean(attended * attended, axis=-1, keepdims=True) + 1e-05)
        outs.append((attended * scale * gains[h * HD : (h + 1) * HD]).astype(jnp.bfloat16))
    head_out = jnp.concatenate(outs, axis=1)
    terms = jnp.dot(head_out, w_out, preferred_element_type=jnp.float32)
    return (tokens.astype(jnp.float32) + scatter_sum(terms)).astype(jnp.bfloat16)


def solution(mesh):
    context = mesh.shape["context"]
    cut = Mesh(mesh.devices.reshape(context // (2 * NEAR), NEAR, 2, SIDE, SIDE), ALL)
    return jax.shard_map(
        local,
        mesh=cut,
        in_specs=(
            P(ALL, None),
            P(),
            P(None, None, ("x", "y")),
            P(("x", "y")),
            P(("x", "y"), None),
        ),
        out_specs=P(ALL, None),
        check_vma=False,
    )
```
